32 devices in a mesh: blk: 8 (over y, x, core), grp: 4 (over z).
Axes of the slice: x: 2, y: 2, z: 4, core: 2. Of those that a mesh axis runs over, the one named last changes fastest.
Arguments:
- tokens: bfloat16 [4096, 4096], P(('blk', 'grp')), may hold values from -6 to 6
- select: int32 [4, 16], P('grp', 'blk'), may hold values from 0 to 4095, as said below
- gates: float32 [4, 16], P('grp', 'blk'), may hold values from 0.1 to 1
- gate_proj: bfloat16 [4, 896, 4096], P('grp', 'blk'), may hold values from -0.09375 to 0.09375
- up_proj: bfloat16 [4, 896, 4096], P('grp', 'blk'), may hold values from -0.09375 to 0.09375
- down_proj: bfloat16 [4, 896, 4096], P('grp', 'blk'), may hold values from -0.1875 to 0.1875
Outputs:
- mixed: bfloat16 [4096, 4096], P(('blk', 'grp'))
The draws below stay inside these ranges and needn't reach their ends.
Inputs may be any that keep to these rules, and one draw needn't show every extreme that they name: `select`: for every expert and every k, the slots k * 2 to (k + 1) * 2 - 1 name 2 different tokens, all from k * 4 * 128 to (k + 1) * 4 * 128 - 1.
All inputs are finite; a program needn't handle non-finite values.
Results may differ from the reference program's by a relative error of at most 0.0095.
Values may be sent and summed in bfloat16 or wider, within the bound.
No kernel may reach another device: no remote copies, remote signals or barrier semaphores. Data moves between devices by JAX's collectives and lax.ppermute only.
A program may use at most 64 MiB of HBM per device.

```python
import math
import jax
import jax.numpy as jnp
from jax import lax

D = 4096
HID_TOTAL = 896
EXP = 4
TOK_DEV = 128
SLOT = 2
CAP = 16
TOKENS = 4096
N_BLK = 8
N_GRP = 4


def draw_select(key, part):
    span = N_GRP * TOK_DEV
    keys = jax.random.split(jax.random.fold_in(key, 17), EXP * N_BLK)
    chosen = jax.vmap(lambda sub: jax.random.permutation(sub, span)[:SLOT])(keys)
    offsets = jnp.arange(EXP * N_BLK, dtype=jnp.int32) % N_BLK * span
    return (chosen.astype(jnp.int32) + offsets[:, None]).reshape(EXP, N_BLK * SLOT).astype(jnp.int32)


def block_levels(rng, extent, cuts, low, top_value):
    def one(position, blocks):
        steps = jax.random.uniform(jax.random.fold_in(jax.random.fold_in(rng, 6), position), (blocks,), jnp.float32, low / len(cuts), top_value / len(cuts))
        return jnp.repeat(jnp.exp(steps), extent[position] // blocks).reshape((-1,) + (1,) * (len(extent) - position - 1))

    level = one(*cuts[0])
    for cut in cuts[1:]:
        level = level * one(*cut)
    return level


def normal_values(stream_key, dims, scale, bound, cuts=(), held_as=jnp.bfloat16):
    result = jax.random.normal(stream_key, dims, jnp.float32) * scale
    if len(cuts) > 0:
        result = block_levels(stream_key, dims, cuts, -0.22, 0.18) * result
    return jnp.clip(result, min=-bound, max=bound).astype(held_as)


def setup_inputs(seed: int = 0) -> dict:
    streams_of = jax.random.split(jax.random.key(seed), 7)
    return {
        "tokens": normal_values(streams_of[0], (TOKENS, D), 1.0, 6.0, ((0, 32),)),
        "select": draw_select(jax.random.fold_in(streams_of[6], 71), 0),
        "gates": jnp.clip(jnp.exp(math.log(1.0) - 2.3025851 * jax.random.uniform(streams_of[2], (EXP, CAP), jnp.float32) ** block_levels(streams_of[2], (EXP, CAP), ((0, 4), (1, 8)), -0.2, 0.2)), 0.1, 1.0),
        "gate_proj": normal_values(streams_of[3], (EXP, HID_TOTAL, D), D ** -0.5, 0.09375, ((0, 4), (1, 8))),
        "up_proj": normal_values(streams_of[4], (EXP, HID_TOTAL, D), D ** -0.5, 0.09375, ((0, 4), (1, 8))),
        "down_proj": normal_values(streams_of[5], (EXP, HID_TOTAL, D), HID_TOTAL ** -0.5, 0.1875, ((0, 4), (1, 8))),
    }


def run_expert(operands):
    rows, w_gate, w_up, w_down = operands
    gate_act = jnp.dot(rows, w_gate.T, preferred_element_type=jnp.float32)
    up_act = jnp.dot(rows, w_up.T, preferred_element_type=jnp.float32)
    hidden = (jax.nn.silu(gate_act) * up_act).astype(jnp.bfloat16)
    return jnp.dot(hidden, w_down, preferred_element_type=jnp.float32).astype(jnp.bfloat16)


def reference(tokens, select, gates, gate_proj, up_proj, down_proj):
    picked = tokens[select.astype(jnp.int32)]
    expert_out = lax.map(run_expert, (picked, gate_proj, up_proj, down_proj))
    weighted = (gates[:, :, None] * expert_out.astype(jnp.float32)).astype(jnp.bfloat16)
    flat_ids = select.reshape(-1).astype(jnp.int32)
    mixed = jnp.zeros((TOKENS, D), jnp.float32).at[flat_ids].add(weighted.reshape(-1, D).astype(jnp.float32))
    return mixed.astype(jnp.bfloat16)
```

```python
import functools

import jax
import jax.numpy as jnp
from jax import lax
from jax.experimental import pallas as pl
from jax.experimental.pallas import tpu as pltpu
from jax.sharding import PartitionSpec as P

KERNEL_VMEM = 16 << 20
NT = (((1,), (1,)), ((), ()))


def general(tokens, select, gates, gate_proj, up_proj, down_proj):
    groups = lax.axis_size("grp")
    tok_dev = tokens.shape[0]
    width = tokens.shape[1]
    slots = select.shape[1]
    first = (lax.axis_index("blk") * groups + lax.axis_index("grp")) * tok_dev
    all_ids = lax.all_gather(select, "grp", axis=0, tiled=True)
    local_ids = all_ids.reshape(-1) - first
    owned = (local_ids[:, None] == jnp.arange(tok_dev, dtype=jnp.int32)[None, :]).astype(
        jnp.bfloat16
    )
    candidates = jnp.dot(owned, tokens, preferred_element_type=jnp.float32)
    arrived = lax.all_to_all(
        candidates.astype(jnp.bfloat16), "grp", split_axis=0, concat_axis=0, tiled=True
    )
    picked = jnp.sum(arrived.reshape(groups, slots, width).astype(jnp.float32), axis=0).astype(
        jnp.bfloat16
    )
    piece = lax.all_gather(picked, "blk", axis=0, tiled=True)
    gate_act = lax.dot_general(piece, gate_proj[0], NT, preferred_element_type=jnp.float32)
    up_act = lax.dot_general(piece, up_proj[0], NT, preferred_element_type=jnp.float32)
    hidden = (jax.nn.silu(gate_act) * up_act).astype(jnp.bfloat16)
    summed = lax.psum_scatter(
        jnp.dot(hidden, down_proj[0], preferred_element_type=jnp.float32),
        "blk",
        scatter_dimension=0,
        tiled=True,
    )
    expert_out = summed.astype(jnp.bfloat16)
    weighted = (gates[0][:, None] * expert_out.astype(jnp.float32)).astype(jnp.bfloat16)
    returned = lax.all_gather(weighted, "grp", axis=0, tiled=True)
    mixed = jnp.dot(owned.T, returned, preferred_element_type=jnp.float32)
    return mixed.astype(jnp.bfloat16)


def pick_kernel(parts, first_ref, *refs):
    ids = refs[:parts]
    own, other = refs[parts : parts + 2]
    outs = refs[parts + 2 : 2 * parts + 2]
    rows_ref = refs[-1]
    per = outs[0].shape[0]
    count = own.shape[0]
    shape = (parts * per, count)
    row = lax.broadcasted_iota(jnp.int32, shape, 0)
    lane = lax.broadcasted_iota(jnp.int32, shape, 1)
    want = jnp.full(shape, -1, jnp.int32)
    for p in range(parts):
        for k in range(per):
            want = jnp.where(row == p * per + k, ids[p][0, k], want)
    mine = (want - first_ref[0] == lane).astype(jnp.float32).astype(jnp.bfloat16)
    theirs = (want - first_ref[1] == lane).astype(jnp.float32).astype(jnp.bfloat16)
    rows_ref[...] = jnp.dot(mine, own[...], preferred_element_type=jnp.float32) + jnp.dot(
        theirs, other[...], preferred_element_type=jnp.float32
    )
    for p in range(parts):
        outs[p][...] = rows_ref[p * per : (p + 1) * per, :].astype(jnp.bfloat16)


def expert_kernel(parts, *refs):
    pieces = refs[:parts]
    gate, up, down = refs[parts : parts + 2], refs[parts + 2 : parts + 4], refs[parts + 4 : parts + 6]
    outs = refs[parts + 6 : 2 * parts + 6]
    rows_ref = refs[-1]
    per = pieces[0].shape[0]
    for p in range(parts):
        rows_ref[p * per : (p + 1) * per, :] = pieces[p][...].astype(jnp.float32)
    rows = rows_ref[...].astype(jnp.bfloat16)
    total = None
    for h in range(2):
        gate_act = lax.dot_general(rows, gate[h][0], NT, preferred_element_type=jnp.float32)
        up_act = lax.dot_general(rows, up[h][0], NT, preferred_element_type=jnp.float32)
        hidden = (gate_act / (1.0 + jnp.exp(-gate_act)) * up_act).astype(jnp.bfloat16)
        term = jnp.dot(hidden, down[h][0], preferred_element_type=jnp.float32)
        total = term if total is None else total + term
    rows_ref[...] = total
    for p in range(parts):
        outs[p][...] = rows_ref[p * per : (p + 1) * per, :].astype(outs[p].dtype)


def in_vmem(count):
    return [pl.BlockSpec(memory_space=pltpu.VMEM)] * count


def in_smem(count):
    return [pl.BlockSpec(memory_space=pltpu.SMEM)] * count


def paired(tokens, select, gates, gate_proj, up_proj, down_proj):
    n_blk, n_grp = lax.axis_size("blk"), lax.axis_size("grp")
    chips = n_blk // 2
    blk, grp = lax.axis_index("blk"), lax.axis_index("grp")
    tok_dev, width = tokens.shape
    per = 2 * select.shape[1]
    both = ("blk", "grp")

    def partner(x):
        return lax.ppermute(x, "blk", [(b, b ^ 1) for b in range(n_blk)])

    def along_grp(x, s):
        pairs = [(b * n_grp + g, (b ^ 1) * n_grp + (g ^ s)) for b in range(n_blk) for g in range(n_grp)]
        return lax.ppermute(x, both, pairs)

    def along_blk(x, s):
        return lax.ppermute(x, "blk", [(b, b ^ (2 * s + 1)) for b in range(n_blk)])

    far_grp = list(range(n_grp - 1, 0, -1))
    far_blk = list(range(chips - 1, 0, -1))

    ids = {0: jnp.concatenate([select, partner(select)], axis=1)}
    for s in far_grp:
        ids[s] = along_grp(ids[0], s)
    other_tokens = partner(tokens)
    weights = []
    for w in (gate_proj, up_proj, down_proj):
        weights += [w, partner(w)]
    chip_gates = jnp.concatenate([gates, partner(gates)], axis=1)

    first = (jnp.stack([blk, blk ^ 1]) * n_grp + grp) * tok_dev
    found = pl.pallas_call(
        functools.partial(pick_kernel, n_grp),
        out_shape=[jax.ShapeDtypeStruct((per, width), jnp.bfloat16)] * n_grp,
        in_specs=in_smem(1 + n_grp) + in_vmem(2),
        out_specs=in_vmem(n_grp),
        scratch_shapes=[pltpu.VMEM((n_grp * per, width), jnp.float32)],
        compiler_params=pltpu.CompilerParams(vmem_limit_bytes=KERNEL_VMEM),
        name="pick",
    )(first, *[ids[s] for s in range(n_grp)], tokens, other_tokens)
    arrived = [found[0]] + [along_grp(found[s], s) for s in far_grp]
    picked = sum(a.astype(jnp.float32) for a in arrived).astype(jnp.bfloat16)

    pieces = {0: picked}
    for s in far_blk:
        pieces[s] = along_blk(picked, s)
    partial = pl.pallas_call(
        functools.partial(expert_kernel, chips),
        out_shape=[jax.ShapeDtypeStruct((per, width), jnp.bfloat16)] * chips,
        in_specs=in_vmem(chips + 6),
        out_specs=in_vmem(chips),
        scratch_shapes=[pltpu.VMEM((chips * per, width), jnp.float32)],
        compiler_params=pltpu.CompilerParams(vmem_limit_bytes=KERNEL_VMEM),
        name="expert",
    )(*[pieces[s] for s in range(chips)], *weights)
    shares = [partial[0]] + [along_blk(partial[s], s) for s in far_blk]
    expert_out = sum(a.astype(jnp.float32) for a in shares).astype(jnp.bfloat16)
    weighted = (chip_gates[0][:, None] * expert_out.astype(jnp.float32)).astype(jnp.bfloat16)

    returned = {0: weighted}
    for s in far_grp:
        returned[s] = along_grp(weighted, s)
    order = range(n_grp)
    local = jnp.concatenate([ids[s][0] for s in order]) - first[0]
    owned = (jnp.arange(tok_dev, dtype=jnp.int32)[:, None] == local[None, :]).astype(jnp.bfloat16)
    mixed = jnp.dot(
        owned,
        jnp.concatenate([returned[s] for s in order], axis=0),
        preferred_element_type=jnp.float32,
    )
    return mixed.astype(jnp.bfloat16)


def cores_side_by_side(mesh):
    n_blk, n_grp = mesh.shape["blk"], mesh.shape["grp"]
    if mesh.axis_names != ("blk", "grp") or n_blk % 2:
        return False
    if any(n & (n - 1) or n > 8 for n in (n_blk // 2, n_grp)):
        return False
    try:
        where = [[tuple(d.coords) for d in row] for row in mesh.devices]
    except AttributeError:
        return False
    return all(where[b] == where[b + 1] for b in range(0, n_blk, 2))


def solution(mesh):
    return jax.shard_map(
        paired if cores_side_by_side(mesh) else general,
        mesh=mesh,
        in_specs=(
            P(("blk", "grp"), None),
            P("grp", "blk"),
            P("grp", "blk"),
            P("grp", "blk", None),
            P("grp", "blk", None),
            P("grp", "blk", None),
        ),
        out_specs=P(("blk", "grp"), None),
        check_vma=False,
    )
```
